128 devices in a mesh: row: 8 (over z, core), col: 16 (over x, y).
Axes of the slice: x: 4, y: 4, z: 4, core: 2. Of those that a mesh axis runs over, the one named last changes fastest.
Arguments:
- tokens: bfloat16 [2048, 8192], P('row', 'col'), may hold values from -6 to 6
- cotangent: bfloat16 [2048, 8192], P('row', 'col'), may hold values from -6 to 6
- gate_weight: bfloat16 [8192, 14336], P('row', 'col'), may hold values from -0.1875 to 0.1875
- up_weight: bfloat16 [8192, 14336], P('row', 'col'), may hold values from -0.1875 to 0.1875
- down_weight: bfloat16 [14336, 8192], P('col', 'row'), may hold values from -0.125 to 0.125
- tile_mask: int32 [64, 112], replicated, may hold values from 0 to 1, as said below
Outputs:
- output: bfloat16 [2048, 8192], P('row', 'col')
- input_grad: bfloat16 [2048, 8192], P('row', 'col')
- gate_grad: bfloat16 [8192, 14336], P('row', 'col')
- up_grad: bfloat16 [8192, 14336], P('row', 'col')
- down_grad: bfloat16 [14336, 8192], P('col', 'row')
The draws below stay inside these ranges and needn't reach their ends.
Inputs may be any that keep to these rules, and one draw needn't show every extreme that they name: `tile_mask`: the mask is made of 8 x 16 blocks of 8 x 7 tiles (block (i, j) holds tile rows i * 8.. and tile columns j * 7..). Each block holds between 2 and 12 ones, some block exactly 12, and the whole mask exactly 896 ones.
All inputs are finite; a program needn't handle non-finite values.
Results may differ from the reference program's by a relative error of at most 0.013.
Values may be sent and summed in bfloat16 or wider, within the bound.
No kernel may reach another device: no remote copies, remote signals or barrier semaphores. Data moves between devices by JAX's collectives and lax.ppermute only.
A program may use at most 192 MiB of HBM per device.

```python
import jax
import jax.numpy as jnp
from jax import lax

D = 8192
FF = 14336
BLK = 128
TOK_DEV = 256
TOKENS = 2048
DT = 64
FT = 112
DTD = 8
FTD = 7
TILES = 56
MEAN = 7
CAP = 12
LOW = 2
NNZ = 896
N_ROW = 8
N_COL = 16


def draw_tile_mask(key, part):
    grid_rows = DT // DTD
    grid_cols = FT // FTD
    devices = grid_rows * grid_cols
    slots = jnp.arange(devices, dtype=jnp.int32)
    base = jnp.where(slots % 4 == 0, CAP, jnp.where(slots % 4 == 1, LOW, MEAN)).astype(jnp.int32)
    counts = jax.random.permutation(jax.random.fold_in(key, 11), base)
    block_keys = jax.random.split(jax.random.fold_in(key, 23), devices)

    def one_block(block_key):
        return jax.random.permutation(block_key, TILES).astype(jnp.int32)
    ranks = jax.vmap(one_block)(block_keys)
    blocks = (ranks < counts[:, None]).astype(jnp.int32).reshape(grid_rows, grid_cols, DTD, FTD)
    return jnp.transpose(blocks, (0, 2, 1, 3)).reshape(DT, FT)


def steps_of(own_key, shape, cuts, smallest, top_value):
    def one(dim, shards_of):
        steps = jax.random.uniform(jax.random.fold_in(jax.random.fold_in(own_key, 6), dim), (shards_of,), jnp.float32, smallest / len(cuts), top_value / len(cuts))
        return jnp.repeat(jnp.exp(steps), shape[dim] // shards_of).reshape((-1,) + (1,) * (len(shape) - dim - 1))

    factor_of = one(*cuts[0])
    for cut in cuts[1:]:
        factor_of = factor_of * one(*cut)
    return factor_of


def centred(own_key, shape, scale, reach, cuts=(), kind=jnp.bfloat16):
    drawn = scale * jax.random.normal(own_key, shape, jnp.float32)
    if cuts:
        drawn = drawn * steps_of(own_key, shape, cuts, -0.22, 0.18)
    return jnp.clip(drawn, -reach, reach).astype(kind)


def setup_inputs(seed: int = 0) -> dict:
    keys = jax.random.split(jax.random.key(seed), 7)
    return {
        "tokens": centred(keys[0], (TOKENS, D), 1.0, 6.0, ((0, 8), (1, 16))),
        "cotangent": centred(keys[1], (TOKENS, D), 1.0, 6.0, ((0, 8), (1, 16))),
        "gate_weight": centred(keys[2], (D, FF), (D // 8) ** -0.5, 0.1875, ((0, 8), (1, 16))),
        "up_weight": centred(keys[3], (D, FF), (D // 8) ** -0.5, 0.1875, ((0, 8), (1, 16))),
        "down_weight": centred(keys[4], (FF, D), (FF // 8) ** -0.5, 0.125, ((0, 16), (1, 8))),
        "tile_mask": draw_tile_mask(jax.random.fold_in(keys[6], 71), 0),
    }


def reference(tokens, cotangent, gate_weight, up_weight, down_weight, tile_mask):
    flat_mask = tile_mask.reshape(-1).astype(jnp.int32)
    places = jnp.arange(DT * FT, dtype=jnp.int32)
    active = jnp.argsort((1 - flat_mask) * (DT * FT) + places)[:NNZ].astype(jnp.int32)
    tile_row = (active // FT).astype(jnp.int32)
    tile_col = (active % FT).astype(jnp.int32)
    group_seg = ((tile_col // FTD) * DT + tile_row).astype(jnp.int32)
    gate_tiles = gate_weight.reshape(DT, BLK, FT, BLK)[tile_row, :, tile_col, :].astype(jnp.float32)
    up_tiles = up_weight.reshape(DT, BLK, FT, BLK)[tile_row, :, tile_col, :].astype(jnp.float32)
    down_tiles = down_weight.reshape(FT, BLK, DT, BLK)[tile_col, :, tile_row, :].astype(jnp.float32)

    def by_cols(parts):
        summed = jax.ops.segment_sum(jnp.swapaxes(parts, 0, 1), tile_col, num_segments=FT)
        return jnp.transpose(summed, (1, 0, 2)).reshape(parts.shape[0], FF)

    def by_groups(parts):
        summed = jax.ops.segment_sum(jnp.swapaxes(parts, 0, 1), group_seg, num_segments=N_COL * DT)
        rounded = lax.optimization_barrier(summed.astype(jnp.bfloat16)).astype(jnp.float32)
        total = jnp.sum(rounded.reshape(N_COL, DT, parts.shape[0], BLK), axis=0)
        return jnp.transpose(total, (1, 0, 2)).reshape(parts.shape[0], D)

    def row_group(pair):
        tok_rows, cot_rows = pair
        count = tok_rows.shape[0]
        token_tiles = tok_rows.reshape(count, DT, BLK)[:, tile_row].astype(jnp.float32)
        gate = by_cols(jnp.einsum('tsk,skn->tsn', token_tiles, gate_tiles))
        upper = by_cols(jnp.einsum('tsk,skn->tsn', token_tiles, up_tiles))
        hidden = (jax.nn.silu(gate) * upper).astype(jnp.bfloat16)
        hidden_tiles = hidden.reshape(count, FT, BLK)[:, tile_col].astype(jnp.float32)
        output = by_groups(jnp.einsum('tsf,sfd->tsd', hidden_tiles, down_tiles)).astype(jnp.bfloat16)
        cot_tiles = cot_rows.reshape(count, DT, BLK)[:, tile_row].astype(jnp.float32)
        hidden_grad = by_cols(jnp.einsum('tsd,sfd->tsf', cot_tiles, down_tiles))
        sigmoid_gate = jax.nn.sigmoid(gate)
        gate_cot = (hidden_grad * upper * sigmoid_gate * (1.0 + gate * (1.0 - sigmoid_gate))).astype(jnp.bfloat16)
        up_cot = (hidden_grad * jax.nn.silu(gate)).astype(jnp.bfloat16)
        gate_back = gate_cot.reshape(count, FT, BLK)[:, tile_col].astype(jnp.float32)
        up_back = up_cot.reshape(count, FT, BLK)[:, tile_col].astype(jnp.float32)
        down_part = jnp.einsum('tsf,tsd->sfd', hidden_tiles, cot_tiles).astype(jnp.bfloat16)
        gate_part = jnp.einsum('tsk,tsn->skn', token_tiles, gate_back).astype(jnp.bfloat16)
        up_part = jnp.einsum('tsk,tsn->skn', token_tiles, up_back).astype(jnp.bfloat16)
        input_terms = jnp.einsum('tsn,skn->tsk', gate_back, gate_tiles) + jnp.einsum('tsn,skn->tsk', up_back, up_tiles)
        input_grad = by_groups(input_terms).astype(jnp.bfloat16)
        return output, input_grad, gate_part, up_part, down_part

    outputs, input_grads, gate_parts, up_parts, down_parts = lax.map(
        row_group, (tokens.reshape(N_ROW, TOK_DEV, D), cotangent.reshape(N_ROW, TOK_DEV, D)))
    gate_sum = jnp.sum(gate_parts.astype(jnp.float32), axis=0).astype(jnp.bfloat16)
    up_sum = jnp.sum(up_parts.astype(jnp.float32), axis=0).astype(jnp.bfloat16)
    down_sum = jnp.sum(down_parts.astype(jnp.float32), axis=0).astype(jnp.bfloat16)
    gate_grad = jnp.zeros((DT, FT, BLK, BLK), jnp.bfloat16).at[tile_row, tile_col].set(gate_sum)
    gate_grad = jnp.transpose(gate_grad, (0, 2, 1, 3)).reshape(D, FF)
    up_grad = jnp.zeros((DT, FT, BLK, BLK), jnp.bfloat16).at[tile_row, tile_col].set(up_sum)
    up_grad = jnp.transpose(up_grad, (0, 2, 1, 3)).reshape(D, FF)
    down_grad = jnp.zeros((FT, DT, BLK, BLK), jnp.bfloat16).at[tile_col, tile_row].set(down_sum)
    down_grad = jnp.transpose(down_grad, (0, 2, 1, 3)).reshape(FF, D)
    return (outputs.reshape(TOKENS, D), input_grads.reshape(TOKENS, D), gate_grad, up_grad, down_grad)
```

```python
import jax
import jax.numpy as jnp
from jax import lax
from jax.experimental import pallas as pl
from jax.experimental.pallas import tpu as pltpu
from jax.sharding import PartitionSpec as P


BLK = 128
CAP = 12
UNROLL = 4
BF = jnp.bfloat16
F32 = jnp.float32
DIST = (0, 3, 1, 2)
MIB = 1 << 20


def shift(axis, k):
    perm = []
    for r in range(8):
        for c in range(16):
            at = {"z": r // 2, "core": r % 2, "x": c // 4, "y": c % 4}
            at[axis] = (at[axis] + k) % (2 if axis == "core" else 4)
            perm.append((r * 16 + c, (at["z"] * 2 + at["core"]) * 16 + at["x"] * 4 + at["y"]))
    return perm


def send(v, axis, k):
    return lax.ppermute(v, ("row", "col"), shift(axis, k))


def ring_gather(v, axis):
    h = v.shape[0] // 2
    a = send(v, axis, 1)
    b = send(v, axis, -1)
    return a, b, send(a[:h], axis, 1), send(b[h:], axis, -1)


def add(*vs):
    total = vs[0].astype(F32)
    for v in vs[1:]:
        total = total + v.astype(F32)
    return total.astype(BF)


def ring_scatter(plus, minus, far_a, far_b, axis):
    h = far_a.shape[0]
    u = send(far_a, axis, 1)
    v = send(far_b, axis, -1)
    plus = jnp.concatenate([add(plus[:h], u), plus[h:]], 0)
    minus = jnp.concatenate([minus[:h], add(minus[h:], v)], 0)
    return send(plus, axis, 1), send(minus, axis, -1)


def place(d):
    return jnp.where(d == 0, 0, jnp.where(d == 1, 2, jnp.where(d == 2, 3, 1)))


def pack_body(mask, where, gate, up, down, out, sems):
    row = where[0] * 2 + where[1]
    col = where[2] * 4 + where[3]

    def copies(slot, i, j):
        r = pl.ds(pl.multiple_of(i * BLK, BLK), BLK)
        c = pl.ds(pl.multiple_of(j * BLK, BLK), BLK)
        return (
            pltpu.make_async_copy(gate.at[r, c], out.at[slot, :, pl.ds(0, BLK)], sems.at[slot, 0]),
            pltpu.make_async_copy(up.at[r, c], out.at[slot, :, pl.ds(BLK, BLK)], sems.at[slot, 1]),
            pltpu.make_async_copy(
                down.at[c, r], out.at[slot, :, pl.ds(2 * BLK, BLK)], sems.at[slot, 2]
            ),
        )

    def tile_row(i, n):
        for j in range(7):
            m = mask[row * 8 + i, col * 7 + j]

            @pl.when((m != 0) & (n < CAP))
            def _(n=n, j=j):
                for copy in copies(n, i, j):
                    copy.start()

            n = n + m
        return n

    n = lax.fori_loop(0, 8, tile_row, jnp.int32(0))

    def finish(s, _):
        for copy in copies(s, 0, 0):
            copy.wait()
        return 0

    lax.fori_loop(0, jnp.minimum(n, CAP), finish, 0)


def pack(mask, where, gate, up, down):
    smem = pl.BlockSpec(memory_space=pltpu.SMEM)
    hbm = pl.BlockSpec(memory_space=pl.ANY)
    return pl.pallas_call(
        pack_body,
        out_shape=jax.ShapeDtypeStruct((CAP, BLK, 3 * BLK), BF),
        in_specs=[smem, smem, hbm, hbm, hbm],
        out_specs=pl.BlockSpec(memory_space=pltpu.VMEM),
        scratch_shapes=[pltpu.SemaphoreType.DMA((CAP, 3))],
        name="pack",
    )(mask, where, gate, up, down)


def plan_body(mask, where, table):
    z, core, x, y = where[0], where[1], where[2], where[3]
    col = x * 4 + y
    total = jnp.int32(0)
    for q in range(8):
        group = ((z + DIST[q % 4]) & 3) * 2 + (core ^ (q // 4))

        def tile_row(i, carry, q=q, group=group):
            total, slot = carry
            owner = group * 2 + i // 4
            sub = i % 4
            px = place((owner // 4 - x) & 3)
            py = place((owner % 4 - y) & 3)
            half = sub // 2
            block = jnp.where(half == 0, py * 4 + px, px * 4 + py)
            pos = half * 32 + block * 2 + sub % 2
            for j in range(7):
                m = mask[group * 8 + i, col * 7 + j]
                table[0, total] = slot
                table[1, total] = pos
                table[2, total] = j
                slot = slot + m
                total = total + m
            return total, slot

        total, _ = lax.fori_loop(0, 8, tile_row, (total, jnp.int32(q * CAP)))
    for k in range(UNROLL):
        table[0, total + k] = 8 * CAP
        table[1, total + k] = 0
        table[2, total + k] = 0
    table[3, 0] = (total + (UNROLL - 1)) // UNROLL


def plan(mask, where):
    smem = pl.BlockSpec(memory_space=pltpu.SMEM)
    return pl.pallas_call(
        plan_body,
        out_shape=jax.ShapeDtypeStruct((4, 128), jnp.int32),
        in_specs=[smem, smem],
        out_specs=smem,
        name="plan",
    )(mask, where)


NT = (((1,), (1,)), ((), ()))
TN = (((0,), (0,)), ((), ()))


def work_body(table, *refs):
    token_parts, refs = refs[:10], refs[10:]
    weight_parts, refs = refs[:10], refs[10:]
    outs, refs = refs[:10], refs[10:]
    grads, refs = refs[:6], refs[6:]
    acts, weights, gu, hidden, hgrad, gucot, rows, sums, gsum, sems = refs
    loads = []
    at = 0
    for ref in token_parts:
        n = ref.shape[0]
        loads.append(pltpu.make_async_copy(ref, acts.at[pl.ds(at, n)], sems.at[len(loads)]))
        at += n
    at = 0
    for ref in weight_parts:
        n = ref.shape[0]
        loads.append(pltpu.make_async_copy(ref, weights.at[pl.ds(at, n)], sems.at[len(loads)]))
        at += n
    for copy in loads:
        copy.start()
    weights[8 * CAP] = jnp.zeros((BLK, 3 * BLK), BF)
    gu[...] = jnp.zeros(gu.shape, F32)
    hgrad[...] = jnp.zeros(hgrad.shape, F32)

    def clear(p, _):
        rows[p] = jnp.zeros((256, BLK), F32)
        return 0

    lax.fori_loop(0, 64, clear, 0)
    for copy in loads:
        copy.wait()
    steps = table[3, 0]

    def entry(k):
        pos = table[1, k]
        return table[0, k], pos, (pos // 2) * 4 + pos % 2, table[2, k]

    def forward(i, _):
        es = [entry(i * UNROLL + k) for k in range(UNROLL)]
        ds = [
            jnp.dot(acts[t], weights[s, :, : 2 * BLK], preferred_element_type=F32)
            for s, _, t, _ in es
        ]
        for (_, _, _, c), d in zip(es, ds):
            gu[c] += d
        return 0

    lax.fori_loop(0, steps, forward, 0)

    def activate(c, _):
        g = gu[c, :, :BLK]
        hidden[c] = (g * jax.nn.sigmoid(g) * gu[c, :, BLK:]).astype(BF)
        return 0

    lax.fori_loop(0, 7, activate, 0)

    def middle(i, _):
        es = [entry(i * UNROLL + k) for k in range(UNROLL)]
        res = []
        for s, _, t, c in es:
            h = hidden[c]
            w = weights[s, :, 2 * BLK :]
            g = acts[t + 2]
            res.append(
                (
                    jnp.dot(h, w, preferred_element_type=F32),
                    lax.dot_general(g, w, NT, preferred_element_type=F32),
                    lax.dot_general(h, g, TN, preferred_element_type=F32),
                )
            )
        for (s, p, _, c), (o, hg, dg) in zip(es, res):
            rows[p] += o
            hgrad[c] += hg
            gsum[s, :, 2 * BLK :] = dg.astype(BF)
        return 0

    lax.fori_loop(0, steps, middle, 0)

    def settle(offset):
        def body(p, _):
            sums[(p // 2) * 4 + p % 2 + offset] = rows[p].astype(BF)
            if offset == 0:
                rows[p] = jnp.zeros((256, BLK), F32)
            return 0

        lax.fori_loop(0, 64, body, 0)

    settle(0)

    def cotangents(c, _):
        g = gu[c, :, :BLK]
        s = jax.nn.sigmoid(g)
        hg = hgrad[c]
        gucot[c, :, :BLK] = (hg * gu[c, :, BLK:] * s * (1.0 + g * (1.0 - s))).astype(BF)
        gucot[c, :, BLK:] = (hg * (g * s)).astype(BF)
        return 0

    lax.fori_loop(0, 7, cotangents, 0)

    def backward(i, _):
        es = [entry(i * UNROLL + k) for k in range(UNROLL)]
        res = []
        for s, _, t, c in es:
            d = gucot[c]
            res.append(
                (
                    lax.dot_general(d, weights[s, :, : 2 * BLK], NT, preferred_element_type=F32),
                    lax.dot_general(acts[t], d, TN, preferred_element_type=F32),
                )
            )
        for (s, p, _, _), (r, wg) in zip(es, res):
            rows[p] += r
            gsum[s, :, : 2 * BLK] = wg.astype(BF)
        return 0

    lax.fori_loop(0, steps, backward, 0)
    settle(2)
    stores = []
    at = 0
    for ref in outs:
        n = ref.shape[0]
        stores.append(pltpu.make_async_copy(sums.at[pl.ds(at, n)], ref, sems.at[len(stores)]))
        at += n
    at = 0
    for ref in grads:
        n = ref.shape[0]
        stores.append(pltpu.make_async_copy(gsum.at[pl.ds(at, n)], ref, sems.at[len(stores)]))
        at += n
    for copy in stores:
        copy.start()
    for copy in stores:
        copy.wait()


def work(table, token_parts, weight_parts):
    smem = pl.BlockSpec(memory_space=pltpu.SMEM)
    hbm = pl.BlockSpec(memory_space=pl.ANY)
    outs = [jax.ShapeDtypeStruct((n, 256, BLK), BF) for n in (16, 16, 16, 8, 8) * 2]
    grads = [jax.ShapeDtypeStruct((n, BLK, 3 * BLK), BF) for n in (12, 12, 12, 6, 6, 48)]
    vmem = pltpu.VMEM
    return pl.pallas_call(
        work_body,
        out_shape=outs + grads,
        in_specs=[smem] + [hbm] * 20,
        out_specs=[hbm] * 16,
        scratch_shapes=[
            vmem((128, 256, BLK), BF),
            vmem((8 * CAP + 1, BLK, 3 * BLK), BF),
            vmem((7, 256, 2 * BLK), F32),
            vmem((7, 256, BLK), BF),
            vmem((7, 256, BLK), F32),
            vmem((7, 256, 2 * BLK), BF),
            vmem((64, 256, BLK), F32),
            vmem((128, 256, BLK), BF),
            vmem((8 * CAP + 1, BLK, 3 * BLK), BF),
            pltpu.SemaphoreType.DMA((20,)),
        ],
        compiler_params=pltpu.CompilerParams(vmem_limit_bytes=56 * MIB),
        name="work",
    )(table, *token_parts, *weight_parts)


def zero_body(*outs):
    for out in outs:
        out[...] = jnp.zeros(out.shape, BF)


def zeros(*shapes):
    return pl.pallas_call(
        zero_body,
        out_shape=[jax.ShapeDtypeStruct(s, BF) for s in shapes],
        name="zeros",
    )()


def unpack_body(mask, where, own, a, b, g0, u0, d0, gate, up, down, total, sems):
    del g0, u0, d0
    row = where[0] * 2 + where[1]
    col = where[2] * 4 + where[3]
    for s in range(CAP):
        total[s] = (own[s].astype(F32) + a[s].astype(F32) + b[s].astype(F32)).astype(BF)

    def copies(slot, i, j):
        r = pl.ds(pl.multiple_of(i * BLK, BLK), BLK)
        c = pl.ds(pl.multiple_of(j * BLK, BLK), BLK)
        return (
            pltpu.make_async_copy(total.at[slot, :, pl.ds(0, BLK)], gate.at[r, c], sems.at[slot, 0]),
            pltpu.make_async_copy(total.at[slot, :, pl.ds(BLK, BLK)], up.at[r, c], sems.at[slot, 1]),
            pltpu.make_async_copy(
                total.at[slot, :, pl.ds(2 * BLK, BLK)], down.at[c, r], sems.at[slot, 2]
            ),
        )

    def tile_row(i, n):
        for j in range(7):
            m = mask[row * 8 + i, col * 7 + j]

            @pl.when((m != 0) & (n < CAP))
            def _(n=n, j=j):
                for copy in copies(n, i, j):
                    copy.start()

            n = n + m
        return n

    n = lax.fori_loop(0, 8, tile_row, jnp.int32(0))

    def finish(s, _):
        for copy in copies(s, 0, 0):
            copy.wait()
        return 0

    lax.fori_loop(0, jnp.minimum(n, CAP), finish, 0)


def unpack(mask, where, own, a, b, blanks):
    smem = pl.BlockSpec(memory_space=pltpu.SMEM)
    hbm = pl.BlockSpec(memory_space=pl.ANY)
    vmem = pl.BlockSpec(memory_space=pltpu.VMEM)
    return pl.pallas_call(
        unpack_body,
        out_shape=[jax.ShapeDtypeStruct(v.shape, BF) for v in blanks],
        in_specs=[smem, smem, vmem, vmem, vmem, hbm, hbm, hbm],
        out_specs=[hbm, hbm, hbm],
        scratch_shapes=[
            pltpu.VMEM((CAP, BLK, 3 * BLK), BF),
            pltpu.SemaphoreType.DMA((CAP, 3)),
        ],
        input_output_aliases={5: 0, 6: 1, 7: 2},
        name="unpack",
    )(mask, where, own, a, b, *blanks)


def on_device(tokens, cotangent, gate_weight, up_weight, down_weight, tile_mask):
    row = lax.axis_index("row")
    col = lax.axis_index("col")
    where = jnp.stack([row // 2, row % 2, col // 4, col % 4]).astype(jnp.int32)

    packed = pack(tile_mask, where, gate_weight, up_weight, down_weight)
    table = plan(tile_mask, where)

    def tiles(v, half):
        v = v[:, half * 256 : half * 256 + 256]
        return [v[:, :BLK], v[:, BLK:]]

    token_parts = []
    for half, (first, second) in enumerate((("x", "y"), ("y", "x"))):
        own = jnp.stack(tiles(tokens, half) + tiles(cotangent, half), 0)
        line = jnp.concatenate([own, *ring_gather(own, first)], 0)
        token_parts += [line, *ring_gather(line, second)]
    a, b, c, d = ring_gather(packed, "z")
    mine = [packed, a, b, c, d]
    weight_parts = mine + [send(v, "core", 1) for v in mine]

    res = work(table, token_parts, weight_parts)
    outs, grads = res[:10], res[10:]

    pair = send(grads[5], "core", 1)
    at = 0
    summed = []
    for v in grads[:5]:
        n = v.shape[0]
        summed.append(add(v, pair[at : at + n]))
        at += n
    own, minus, plus, far_a, far_b = summed
    from_minus, from_plus = ring_scatter(plus, minus, far_a, far_b, "z")
    blanks = zeros(gate_weight.shape, up_weight.shape, down_weight.shape)
    gate_grad, up_grad, down_grad = unpack(tile_mask, where, own, from_minus, from_plus, blanks)

    ends = []
    for half, (first, second) in enumerate((("y", "x"), ("x", "y"))):
        own, minus, plus, far_a, far_b = outs[half * 5 : half * 5 + 5]
        p, m = ring_scatter(plus, minus, far_a, far_b, first)
        line = [add(own[k * 4 : k * 4 + 4], p[k * 4 : k * 4 + 4], m[k * 4 : k * 4 + 4]) for k in range(4)]
        p, m = ring_scatter(line[2], line[1], line[3][:2], line[3][2:], second)
        ends.append(add(line[0], p, m))
    output = jnp.concatenate([ends[0][0], ends[0][1], ends[1][0], ends[1][1]], 1)
    input_grad = jnp.concatenate([ends[0][2], ends[0][3], ends[1][2], ends[1][3]], 1)
    return output, input_grad, gate_grad, up_grad, down_grad


def solution(mesh):
    spec = P("row", "col")
    turned = P("col", "row")
    return jax.shard_map(
        on_device,
        mesh=mesh,
        in_specs=(spec, spec, spec, spec, turned, P()),
        out_specs=(spec, spec, spec, spec, turned),
        check_vma=False,
    )
```

```python
import jax
import jax.numpy as jnp
from jax import lax
from jax.experimental import pallas as pl
from jax.experimental.pallas import tpu as pltpu
from jax.sharding import PartitionSpec as P


BLK = 128
CAP = 12
UNROLL = 4
BF = jnp.bfloat16
F32 = jnp.float32
DIST = (0, 3, 1, 2)
MIB = 1 << 20


def shift(axis, k):
    perm = []
    for r in range(8):
        for c in range(16):
            at = {"z": r // 2, "core": r % 2, "x": c // 4, "y": c % 4}
            at[axis] = (at[axis] + k) % (2 if axis == "core" else 4)
            perm.append((r * 16 + c, (at["z"] * 2 + at["core"]) * 16 + at["x"] * 4 + at["y"]))
    return perm


def send(v, axis, k):
    return lax.ppermute(v, ("row", "col"), shift(axis, k))


def ring_gather(v, axis):
    h = v.shape[0] // 2
    a = send(v, axis, 1)
    b = send(v, axis, -1)
    c, d = a[:h], b[h:]
    return a, b, send(c, axis, 1), send(d, axis, -1)


def gather_four(v, axis):
    return [v, send(v, axis, 1), send(v, axis, -1), send(v, axis, 2)]


def scatter_four(parts, axis):
    own, minus, plus, far = parts
    return [own, send(minus, axis, -1), send(plus, axis, 1), send(far, axis, 2)]


def add(*vs):
    total = vs[0].astype(F32)
    for v in vs[1:]:
        total = total + v.astype(F32)
    return total.astype(BF)


def place(d):
    return jnp.where(d == 0, 0, jnp.where(d == 1, 2, jnp.where(d == 2, 3, 1)))


def pack_body(mask, where, gate, up, down, out, sems):
    row = where[0] * 2 + where[1]
    col = where[2] * 4 + where[3]

    def copies(slot, i, j):
        r = pl.ds(pl.multiple_of(i * BLK, BLK), BLK)
        c = pl.ds(pl.multiple_of(j * BLK, BLK), BLK)
        return (
            pltpu.make_async_copy(gate.at[r, c], out.at[slot, :, pl.ds(0, BLK)], sems.at[slot, 0]),
            pltpu.make_async_copy(up.at[r, c], out.at[slot, :, pl.ds(BLK, BLK)], sems.at[slot, 1]),
            pltpu.make_async_copy(
                down.at[c, r], out.at[slot, :, pl.ds(2 * BLK, BLK)], sems.at[slot, 2]
            ),
        )

    def tile_row(i, n):
        for j in range(7):
            m = mask[row * 8 + i, col * 7 + j]

            @pl.when((m != 0) & (n < CAP))
            def _(n=n, j=j):
                for copy in copies(n, i, j):
                    copy.start()

            n = n + m
        return n

    n = lax.fori_loop(0, 8, tile_row, jnp.int32(0))

    def finish(s, _):
        for copy in copies(s, 0, 0):
            copy.wait()
        return 0

    lax.fori_loop(0, jnp.minimum(n, CAP), finish, 0)


def pack(mask, where, gate, up, down):
    smem = pl.BlockSpec(memory_space=pltpu.SMEM)
    hbm = pl.BlockSpec(memory_space=pl.ANY)
    return pl.pallas_call(
        pack_body,
        out_shape=jax.ShapeDtypeStruct((CAP, BLK, 3 * BLK), BF),
        in_specs=[smem, smem, hbm, hbm, hbm],
        out_specs=pl.BlockSpec(memory_space=pltpu.VMEM),
        scratch_shapes=[pltpu.SemaphoreType.DMA((CAP, 3))],
        name="pack",
    )(mask, where, gate, up, down)


def plan_body(mask, where, table):
    z, core, x, y = where[0], where[1], where[2], where[3]
    col = x * 4 + y
    total = jnp.int32(0)
    for q in range(8):
        group = ((z + DIST[q % 4]) & 3) * 2 + (core ^ (q // 4))

        def tile_row(i, carry, q=q, group=group):
            total, slot = carry
            owner = group * 2 + i // 4
            sub = i % 4
            px = place((owner // 4 - x) & 3)
            py = place((owner % 4 - y) & 3)
            at_x_y = (py * 4 + px) * 4 + sub
            at_y_x = (px * 4 + py) * 4 + sub
            for j in range(7):
                m = mask[group * 8 + i, col * 7 + j]
                table[0, total] = slot
                table[1, total] = at_x_y
                table[2, total] = at_y_x
                table[3, total] = j
                slot = slot + m
                total = total + m
            return total, slot

        total, _ = lax.fori_loop(0, 8, tile_row, (total, jnp.int32(q * CAP)))
    for k in range(UNROLL):
        table[0, total + k] = 8 * CAP
        table[1, total + k] = 0
        table[2, total + k] = 0
        table[3, total + k] = 0
    table[4, 0] = (total + (UNROLL - 1)) // UNROLL


def plan(mask, where):
    smem = pl.BlockSpec(memory_space=pltpu.SMEM)
    return pl.pallas_call(
        plan_body,
        out_shape=jax.ShapeDtypeStruct((8, 128), jnp.int32),
        in_specs=[smem, smem],
        out_specs=smem,
        name="plan",
    )(mask, where)


NT = (((1,), (1,)), ((), ()))
TN = (((0,), (0,)), ((), ()))


def fetch(parts, buffer, sems, first):
    copies = []
    at = 0
    for ref in parts:
        n = ref.shape[0]
        copies.append(pltpu.make_async_copy(ref, buffer.at[pl.ds(at, n)], sems.at[first + len(copies)]))
        at += n
    for copy in copies:
        copy.start()
    return copies


def store(parts, buffer, sems, first):
    copies = []
    at = 0
    for ref in parts:
        n = ref.shape[0]
        copies.append(pltpu.make_async_copy(buffer.at[pl.ds(at, n)], ref, sems.at[first + len(copies)]))
        at += n
    for copy in copies:
        copy.start()
    return copies


def wait(copies):
    for copy in copies:
        copy.wait()


def clear(ref):
    def body(p, _):
        ref[p] = jnp.zeros(ref.shape[1:], ref.dtype)
        return 0

    lax.fori_loop(0, ref.shape[0], body, 0)


def settle(rows, sums):
    def body(p, _):
        sums[p] = rows[p].astype(BF)
        return 0

    lax.fori_loop(0, 64, body, 0)


def forward_body(table, *refs):
    token_parts, refs = refs[:4], refs[4:]
    weight_parts, refs = refs[:10], refs[10:]
    outs, refs = refs[:4], refs[4:]
    gu, hidden, acts, weights, rows, sums, sems = refs
    loads = fetch(token_parts, acts, sems, 0) + fetch(weight_parts, weights, sems, 4)
    weights[8 * CAP] = jnp.zeros((BLK, 3 * BLK), BF)
    clear(gu)
    clear(rows)
    wait(loads)
    steps = table[4, 0]

    def entry(k):
        return table[0, k], table[1, k], table[3, k]

    def forward(i, _):
        es = [entry(i * UNROLL + k) for k in range(UNROLL)]
        ds = [
            jnp.dot(acts[t], weights[s, :, : 2 * BLK], preferred_element_type=F32)
            for s, t, _ in es
        ]
        for (_, _, c), d in zip(es, ds):
            gu[c] += d
        return 0

    lax.fori_loop(0, steps, forward, 0)

    def activate(c, _):
        g = gu[c, :, :BLK]
        hidden[c] = (g * jax.nn.sigmoid(g) * gu[c, :, BLK:]).astype(BF)
        return 0

    lax.fori_loop(0, 7, activate, 0)

    def output(i, _):
        es = [entry(i * UNROLL + k) for k in range(UNROLL)]
        ds = [
            jnp.dot(hidden[c], weights[s, :, 2 * BLK :], preferred_element_type=F32)
            for s, _, c in es
        ]
        for (_, t, _), d in zip(es, ds):
            rows[t] += d
        return 0

    lax.fori_loop(0, steps, output, 0)
    settle(rows, sums)
    wait(store(outs, sums, sems, 0))


SMEM = pl.BlockSpec(memory_space=pltpu.SMEM)
HBM = pl.BlockSpec(memory_space=pl.ANY)
IN_VMEM = pl.BlockSpec(memory_space=pltpu.VMEM)


def cost(tiles, moved):
    return pl.CostEstimate(
        flops=tiles * 8 * 2 * 256 * BLK * BLK, bytes_accessed=moved, transcendentals=0
    )


def part_shapes(*tail):
    return [jax.ShapeDtypeStruct((16, *tail), BF)] * 4


def forward_work(table, token_parts, weight_parts):
    vmem = pltpu.VMEM
    return pl.pallas_call(
        forward_body,
        out_shape=part_shapes(256, BLK)
        + [jax.ShapeDtypeStruct((7, 256, 2 * BLK), F32), jax.ShapeDtypeStruct((7, 256, BLK), BF)],
        in_specs=[SMEM] + [HBM] * 14,
        out_specs=[HBM] * 4 + [IN_VMEM] * 2,
        scratch_shapes=[
            vmem((64, 256, BLK), BF),
            vmem((8 * CAP + 1, BLK, 3 * BLK), BF),
            vmem((64, 256, BLK), F32),
            vmem((64, 256, BLK), BF),
            pltpu.SemaphoreType.DMA((14,)),
        ],
        compiler_params=pltpu.CompilerParams(vmem_limit_bytes=36 * MIB),
        cost_estimate=cost(56 * 3 * 4, 20 * MIB),
        name="forward",
    )(table, *token_parts, *weight_parts)


def input_body(table, gu, hidden, *refs):
    cot_parts, refs = refs[:4], refs[4:]
    weight_parts, refs = refs[:10], refs[10:]
    outs, refs = refs[:4], refs[4:]
    grads, refs = refs[:5], refs[5:]
    gucot, cots, weights, hgrad, rows, sums, gsum, sems = refs
    loads = fetch(cot_parts, cots, sems, 0) + fetch(weight_parts, weights, sems, 4)
    weights[8 * CAP] = jnp.zeros((BLK, 3 * BLK), BF)
    clear(hgrad)
    clear(rows)
    wait(loads)
    steps = table[4, 0]

    def entry(k):
        return table[0, k], table[2, k], table[3, k]

    def middle(i, _):
        es = [entry(i * UNROLL + k) for k in range(UNROLL)]
        res = []
        for s, t, c in es:
            g = cots[t]
            res.append(
                (
                    lax.dot_general(g, weights[s, :, 2 * BLK :], NT, preferred_element_type=F32),
                    lax.dot_general(hidden[c], g, TN, preferred_element_type=F32),
                )
            )
        for (s, _, c), (hg, dg) in zip(es, res):
            hgrad[c] += hg
            gsum[s] = dg.astype(BF)
        return 0

    lax.fori_loop(0, steps, middle, 0)
    stores = store(grads, gsum, sems, 0)

    def cotangents(c, _):
        g = gu[c, :, :BLK]
        s = jax.nn.sigmoid(g)
        hg = hgrad[c]
        gucot[c, :, :BLK] = (hg * gu[c, :, BLK:] * s * (1.0 + g * (1.0 - s))).astype(BF)
        gucot[c, :, BLK:] = (hg * (g * s)).astype(BF)
        return 0

    lax.fori_loop(0, 7, cotangents, 0)

    def backward(i, _):
        es = [entry(i * UNROLL + k) for k in range(UNROLL)]
        res = [
            lax.dot_general(gucot[c], weights[s, :, : 2 * BLK], NT, preferred_element_type=F32)
            for s, _, c in es
        ]
        for (_, t, _), r in zip(es, res):
            rows[t] += r
        return 0

    lax.fori_loop(0, steps, backward, 0)
    settle(rows, sums)
    wait(stores + store(outs, sums, sems, 5))


def grad_shapes(width):
    return [jax.ShapeDtypeStruct((n, BLK, width), BF) for n in (12, 12, 12, 12, 48)]


def input_work(table, gu, hidden, cot_parts, weight_parts):
    vmem = pltpu.VMEM
    return pl.pallas_call(
        input_body,
        out_shape=part_shapes(256, BLK)
        + grad_shapes(BLK)
        + [jax.ShapeDtypeStruct((7, 256, 2 * BLK), BF)],
        in_specs=[SMEM] + [IN_VMEM] * 2 + [HBM] * 14,
        out_specs=[HBM] * 9 + [IN_VMEM],
        scratch_shapes=[
            vmem((64, 256, BLK), BF),
            vmem((8 * CAP + 1, BLK, 3 * BLK), BF),
            vmem((7, 256, BLK), F32),
            vmem((64, 256, BLK), F32),
            vmem((64, 256, BLK), BF),
            vmem((8 * CAP + 1, BLK, BLK), BF),
            pltpu.SemaphoreType.DMA((14,)),
        ],
        compiler_params=pltpu.CompilerParams(vmem_limit_bytes=44 * MIB),
        cost_estimate=cost(56 * 4 * 4, 22 * MIB),
        name="inputs",
    )(table, gu, hidden, *cot_parts, *weight_parts)


def grad_body(table, gucot, *refs):
    token_parts, refs = refs[:4], refs[4:]
    grads, refs = refs[:5], refs[5:]
    acts, gsum, sems = refs
    wait(fetch(token_parts, acts, sems, 0))
    steps = table[4, 0]

    def backward(i, _):
        es = [
            (table[0, i * UNROLL + k], table[1, i * UNROLL + k], table[3, i * UNROLL + k])
            for k in range(UNROLL)
        ]
        res = [
            lax.dot_general(acts[t], gucot[c], TN, preferred_element_type=F32) for _, t, c in es
        ]
        for (s, _, _), r in zip(es, res):
            gsum[s] = r.astype(BF)
        return 0

    lax.fori_loop(0, steps, backward, 0)
    wait(store(grads, gsum, sems, 0))


def grad_work(table, gucot, token_parts):
    vmem = pltpu.VMEM
    return pl.pallas_call(
        grad_body,
        out_shape=grad_shapes(2 * BLK),
        in_specs=[SMEM, IN_VMEM] + [HBM] * 4,
        out_specs=[HBM] * 5,
        scratch_shapes=[
            vmem((64, 256, BLK), BF),
            vmem((8 * CAP + 1, BLK, 2 * BLK), BF),
            pltpu.SemaphoreType.DMA((5,)),
        ],
        compiler_params=pltpu.CompilerParams(vmem_limit_bytes=20 * MIB),
        cost_estimate=cost(56 * 2 * 4, 10 * MIB),
        name="grads",
    )(table, gucot, *token_parts)


def zero_body(*outs):
    for out in outs:
        out[...] = jnp.zeros(out.shape, BF)


def zeros(*shapes):
    return pl.pallas_call(
        zero_body,
        out_shape=[jax.ShapeDtypeStruct(s, BF) for s in shapes],
        name="zeros",
    )()


def unpack_body(mask, where, *refs):
    downs, refs = refs[:4], refs[4:]
    pairs, refs = refs[:4], refs[4:]
    gate, up, down, total, sems = refs[3:]
    row = where[0] * 2 + where[1]
    col = where[2] * 4 + where[3]
    for s in range(CAP):
        for parts, lanes in ((pairs, slice(0, 2 * BLK)), (downs, slice(2 * BLK, 3 * BLK))):
            v = parts[0][s].astype(F32)
            for part in parts[1:]:
                v = v + part[s].astype(F32)
            total[s, :, lanes] = v.astype(BF)

    def copies(slot, i, j):
        r = pl.ds(pl.multiple_of(i * BLK, BLK), BLK)
        c = pl.ds(pl.multiple_of(j * BLK, BLK), BLK)
        return (
            pltpu.make_async_copy(total.at[slot, :, pl.ds(0, BLK)], gate.at[r, c], sems.at[slot, 0]),
            pltpu.make_async_copy(total.at[slot, :, pl.ds(BLK, BLK)], up.at[r, c], sems.at[slot, 1]),
            pltpu.make_async_copy(
                total.at[slot, :, pl.ds(2 * BLK, BLK)], down.at[c, r], sems.at[slot, 2]
            ),
        )

    def tile_row(i, n):
        for j in range(7):
            m = mask[row * 8 + i, col * 7 + j]

            @pl.when((m != 0) & (n < CAP))
            def _(n=n, j=j):
                for copy in copies(n, i, j):
                    copy.start()

            n = n + m
        return n

    n = lax.fori_loop(0, 8, tile_row, jnp.int32(0))

    def finish(s, _):
        for copy in copies(s, 0, 0):
            copy.wait()
        return 0

    lax.fori_loop(0, jnp.minimum(n, CAP), finish, 0)


def unpack(mask, where, downs, pairs, blanks):
    return pl.pallas_call(
        unpack_body,
        out_shape=[jax.ShapeDtypeStruct(v.shape, BF) for v in blanks],
        in_specs=[SMEM, SMEM] + [IN_VMEM] * 8 + [HBM] * 3,
        out_specs=[HBM, HBM, HBM],
        scratch_shapes=[
            pltpu.VMEM((CAP, BLK, 3 * BLK), BF),
            pltpu.SemaphoreType.DMA((CAP, 3)),
        ],
        input_output_aliases={10: 0, 11: 1, 12: 2},
        name="unpack",
    )(mask, where, *downs, *pairs, *blanks)


def on_device(tokens, cotangent, gate_weight, up_weight, down_weight, tile_mask):
    row = lax.axis_index("row")
    col = lax.axis_index("col")
    where = jnp.stack([row // 2, row % 2, col // 4, col % 4]).astype(jnp.int32)

    packed = pack(tile_mask, where, gate_weight, up_weight, down_weight)
    table = plan(tile_mask, where)

    def gather(v, first, second):
        own = jnp.stack([v[:, k * BLK : k * BLK + BLK] for k in range(4)], 0)
        line = jnp.concatenate(gather_four(own, first), 0)
        return gather_four(line, second)

    def finish(got, axis):
        line = [add(*(v[k * 4 : k * 4 + 4] for v in got)) for k in range(4)]
        end = add(*scatter_four(line, axis))
        return jnp.concatenate([end[k] for k in range(4)], 1)

    def row_sums(grads):
        pair = send(grads[4], "core", 1)
        return [add(v, pair[k * CAP : k * CAP + CAP]) for k, v in enumerate(grads[:4])]

    token_parts = gather(tokens, "x", "y")
    a, b, c, d = ring_gather(packed, "z")
    mine = [packed, a, b, c, d]
    weight_parts = mine + [send(v, "core", 1) for v in mine]
    cot_parts = gather(cotangent, "y", "x")

    *outs, gu, hidden = forward_work(table, token_parts, weight_parts)
    outs = scatter_four(outs, "y")
    res = input_work(table, gu, hidden, cot_parts, weight_parts)
    ins, downs, gucot = res[:4], res[4:9], res[9]
    ins = scatter_four(ins, "x")
    downs = scatter_four(row_sums(downs), "z")
    pairs = grad_work(table, gucot, token_parts)
    pairs = scatter_four(row_sums(pairs), "z")
    output = finish(outs, "x")
    blanks = zeros(gate_weight.shape, up_weight.shape, down_weight.shape)
    gate_grad, up_grad, down_grad = unpack(tile_mask, where, downs, pairs, blanks)
    input_grad = finish(ins, "y")
    return output, input_grad, gate_grad, up_grad, down_grad


def solution(mesh):
    spec = P("row", "col")
    turned = P("col", "row")

    return jax.shard_map(
        on_device,
        mesh=mesh,
        in_specs=(spec, spec, spec, spec, turned, P()),
        out_specs=(spec, spec, spec, spec, turned),
        check_vma=False,
    )
```

```python
import jax
import jax.numpy as jnp
from jax import lax
from jax.experimental import pallas as pl
from jax.experimental.pallas import tpu as pltpu
from jax.sharding import PartitionSpec as P


BLK = 128
CAP = 12
UNROLL = 4
BF = jnp.bfloat16
F32 = jnp.float32
DIST = (0, 3, 1, 2)
MIB = 1 << 20


def shift(axis, k):
    perm = []
    for r in range(8):
        for c in range(16):
            at = {"z": r // 2, "core": r % 2, "x": c // 4, "y": c % 4}
            at[axis] = (at[axis] + k) % (2 if axis == "core" else 4)
            perm.append((r * 16 + c, (at["z"] * 2 + at["core"]) * 16 + at["x"] * 4 + at["y"]))
    return perm


def send(v, axis, k):
    return lax.ppermute(v, ("row", "col"), shift(axis, k))


def ring_gather(v, axis):
    h = v.shape[0] // 2
    a = send(v, axis, 1)
    b = send(v, axis, -1)
    c, d = a[:h], b[h:]
    return a, b, send(c, axis, 1), send(d, axis, -1)


def gather_four(v, axis):
    return [v, send(v, axis, 1), send(v, axis, -1), send(v, axis, 2)]


def scatter_four(parts, axis):
    own, minus, plus, far = parts
    return [own, send(minus, axis, -1), send(plus, axis, 1), send(far, axis, 2)]


def add(*vs):
    total = vs[0].astype(F32)
    for v in vs[1:]:
        total = total + v.astype(F32)
    return total.astype(BF)


def place(d):
    return jnp.where(d == 0, 0, jnp.where(d == 1, 2, jnp.where(d == 2, 3, 1)))


def place_back(p):
    return jnp.where(p == 0, 0, jnp.where(p == 1, 3, jnp.where(p == 2, 1, 2)))


def pack_body(mask, where, gate, up, down, out, sems):
    row = where[0] * 2 + where[1]
    col = where[2] * 4 + where[3]

    def copies(slot, i, j):
        r = pl.ds(pl.multiple_of(i * BLK, BLK), BLK)
        c = pl.ds(pl.multiple_of(j * BLK, BLK), BLK)
        return (
            pltpu.make_async_copy(gate.at[r, c], out.at[slot, :, pl.ds(0, BLK)], sems.at[slot, 0]),
            pltpu.make_async_copy(up.at[r, c], out.at[slot, :, pl.ds(BLK, BLK)], sems.at[slot, 1]),
            pltpu.make_async_copy(
                down.at[c, r], out.at[slot, :, pl.ds(2 * BLK, BLK)], sems.at[slot, 2]
            ),
        )

    def tile_col(j, n):
        for i in range(8):
            m = mask[row * 8 + i, col * 7 + j]

            @pl.when((m != 0) & (n < CAP))
            def _(n=n, i=i):
                for copy in copies(n, i, j):
                    copy.start()

            n = n + m
        return n

    n = lax.fori_loop(0, 7, tile_col, jnp.int32(0))

    def finish(s, _):
        for copy in copies(s, 0, 0):
            copy.wait()
        return 0

    lax.fori_loop(0, jnp.minimum(n, CAP), finish, 0)


def pack(mask, where, gate, up, down):
    smem = pl.BlockSpec(memory_space=pltpu.SMEM)
    hbm = pl.BlockSpec(memory_space=pl.ANY)
    return pl.pallas_call(
        pack_body,
        out_shape=jax.ShapeDtypeStruct((CAP, BLK, 3 * BLK), BF),
        in_specs=[smem, smem, hbm, hbm, hbm],
        out_specs=pl.BlockSpec(memory_space=pltpu.VMEM),
        scratch_shapes=[pltpu.SemaphoreType.DMA((CAP, 3))],
        name="pack",
    )(mask, where, gate, up, down)


def plan_body(mask, where, table):
    z, core, x, y = where[0], where[1], where[2], where[3]
    col = x * 4 + y

    def spot(k, _):
        q = k // 8
        d = place_back(q % 4)
        owner = (((z + d) & 3) * 2 + (core ^ (q // 4))) * 2 + (k % 8) // 4
        px = place((owner // 4 - x) & 3)
        py = place((owner % 4 - y) & 3)
        table[5, k] = (py * 4 + px) * 4 + k % 4
        table[6, k] = (px * 4 + py) * 4 + k % 4
        return 0

    lax.fori_loop(0, 64, spot, 0)
    groups = [((z + DIST[q % 4]) & 3) * 2 + (core ^ (q // 4)) for q in range(8)]

    def tile_col(j, carry):
        total, slots = carry[0], list(carry[1:])
        for q in range(8):
            for i in range(8):
                m = mask[groups[q] * 8 + i, col * 7 + j]
                table[0, total] = slots[q]
                table[1, total] = table[5, q * 8 + i]
                table[2, total] = table[6, q * 8 + i]
                table[3, total] = j
                slots[q] = slots[q] + m
                total = total + m
        for k in range(UNROLL):
            table[0, total + k] = 8 * CAP
            table[1, total + k] = 0
            table[2, total + k] = 0
            table[3, total + k] = j
        total = ((total + (UNROLL - 1)) // UNROLL) * UNROLL
        return (total, *slots)

    start = (jnp.int32(0), *(jnp.int32(q * CAP) for q in range(8)))
    total = lax.fori_loop(0, 7, tile_col, start)[0]
    for k in range(UNROLL):
        table[0, total + k] = 8 * CAP
        table[1, total + k] = 0
        table[2, total + k] = 0
        table[3, total + k] = 0
    table[4, 0] = (total // UNROLL + 1) // 2


def plan(mask, where):
    smem = pl.BlockSpec(memory_space=pltpu.SMEM)
    return pl.pallas_call(
        plan_body,
        out_shape=jax.ShapeDtypeStruct((8, 128), jnp.int32),
        in_specs=[smem, smem],
        out_specs=smem,
        name="plan",
    )(mask, where)


SMEM = pl.BlockSpec(memory_space=pltpu.SMEM)
HBM = pl.BlockSpec(memory_space=pl.ANY)
IN_VMEM = pl.BlockSpec(memory_space=pltpu.VMEM)
NT = (((1,), (1,)), ((), ()))
TN = (((0,), (0,)), ((), ()))


def fetch(parts, buffer, sems, first):
    copies = []
    at = 0
    for ref in parts:
        n = ref.shape[0]
        copies.append(pltpu.make_async_copy(ref, buffer.at[pl.ds(at, n)], sems.at[first + len(copies)]))
        at += n
    for copy in copies:
        copy.start()
    return copies


def store(parts, buffer, sems, first):
    copies = []
    at = 0
    for ref in parts:
        n = ref.shape[0]
        copies.append(pltpu.make_async_copy(buffer.at[pl.ds(at, n)], ref, sems.at[first + len(copies)]))
        at += n
    for copy in copies:
        copy.start()
    return copies


def wait(copies):
    for copy in copies:
        copy.wait()


def clear(ref):
    def body(p, _):
        ref[p] = jnp.zeros(ref.shape[1:], ref.dtype)
        return 0

    lax.fori_loop(0, ref.shape[0], body, 0)


def settle(rows, sums, parts, sems, first):
    copies = []
    for k, part in enumerate(parts):
        def body(p, _):
            for r in range(4):
                sums[p * 4 + r] = rows[p * 4 + r].astype(BF)
            return 0

        lax.fori_loop(k * 4, k * 4 + 4, body, 0)
        copies.append(pltpu.make_async_copy(sums.at[pl.ds(k * 16, 16)], part, sems.at[first + k]))
        copies[-1].start()
    return copies


def step(table, i, spots):
    at = i * UNROLL
    return (
        [table[0, at + k] for k in range(UNROLL)],
        [table[spots, at + k] for k in range(UNROLL)],
        table[3, at],
    )


def side(values, axis):
    return [jnp.concatenate(values[k : k + 2], axis) for k in range(0, UNROLL, 2)]


GU = slice(0, 2 * BLK)
DOWN = slice(2 * BLK, 3 * BLK)


def stage_body(*refs):
    parts, out, sems = refs[:10], refs[10], refs[11]
    copies = fetch(parts, out, sems, 0)
    out[8 * CAP] = jnp.zeros((BLK, 3 * BLK), BF)
    wait(copies)


def stage(parts):
    return pl.pallas_call(
        stage_body,
        out_shape=jax.ShapeDtypeStruct((8 * CAP + 1, BLK, 3 * BLK), BF),
        in_specs=[HBM] * 10,
        out_specs=IN_VMEM,
        scratch_shapes=[pltpu.SemaphoreType.DMA((10,))],
        name="stage",
    )(*parts)


def in_pairs(steps, body):
    def turn(i, _):
        body(i * 2)
        body(i * 2 + 1)
        return 0

    lax.fori_loop(0, steps, turn, 0)


def forward_body(table, *refs):
    token_parts, refs = refs[:4], refs[4:]
    weights, refs = refs[0], refs[1:]
    outs, refs = refs[:4], refs[4:]
    gu, hidden, acts, rows, sums, sems = refs
    loads = fetch(token_parts, acts, sems, 0)
    clear(gu)
    clear(rows)
    wait(loads)
    steps = table[4, 0]

    def forward(i):
        slots, spots, c = step(table, i, 1)
        lhs = side([acts[t] for t in spots], 1)
        rhs = side([weights[s, :, GU] for s in slots], 0)
        gu[c] += sum(jnp.dot(a, b, preferred_element_type=F32) for a, b in zip(lhs, rhs))

    in_pairs(steps, forward)

    def activate(c, _):
        g = gu[c, :, :BLK]
        hidden[c] = (g * jax.nn.sigmoid(g) * gu[c, :, BLK:]).astype(BF)
        return 0

    lax.fori_loop(0, 7, activate, 0)

    def output(i):
        slots, spots, c = step(table, i, 1)
        h = hidden[c]
        rhs = side([weights[s, :, DOWN] for s in slots], 1)
        ds = [jnp.dot(h, b, preferred_element_type=F32) for b in rhs]
        for k, t in enumerate(spots):
            rows[t] += ds[k // 2][:, (k % 2) * BLK : (k % 2) * BLK + BLK]

    in_pairs(steps, output)
    wait(settle(rows, sums, outs, sems, 0))


def cost(tiles, moved):
    return pl.CostEstimate(
        flops=tiles * 8 * 2 * 256 * BLK * BLK, bytes_accessed=moved, transcendentals=0
    )


def part_shapes(*tail):
    return [jax.ShapeDtypeStruct((16, *tail), BF)] * 4


def forward_work(table, token_parts, weights):
    vmem = pltpu.VMEM
    return pl.pallas_call(
        forward_body,
        out_shape=part_shapes(256, BLK)
        + [jax.ShapeDtypeStruct((7, 256, 2 * BLK), F32), jax.ShapeDtypeStruct((7, 256, BLK), BF)],
        in_specs=[SMEM] + [HBM] * 4 + [IN_VMEM],
        out_specs=[HBM] * 4 + [IN_VMEM] * 2,
        scratch_shapes=[
            vmem((64, 256, BLK), BF),
            vmem((64, 256, BLK), F32),
            vmem((64, 256, BLK), BF),
            pltpu.SemaphoreType.DMA((14,)),
        ],
        compiler_params=pltpu.CompilerParams(vmem_limit_bytes=20 * MIB),
        cost_estimate=cost(56 * 3 * 4, 20 * MIB),
        name="forward",
    )(table, *token_parts, weights)


def input_body(table, gu, hidden, *refs):
    cot_parts, refs = refs[:4], refs[4:]
    weights, refs = refs[0], refs[1:]
    outs, refs = refs[:4], refs[4:]
    grads, refs = refs[:5], refs[5:]
    gucot, cots, hgrad, rows, sums, gsum, sems = refs
    loads = fetch(cot_parts, cots, sems, 0)
    clear(hgrad)
    clear(rows)
    wait(loads)
    steps = table[4, 0]

    def middle(i):
        slots, spots, c = step(table, i, 2)
        gs = [cots[t] for t in spots]
        lhs = side(gs, 1)
        rhs = side([weights[s, :, DOWN] for s in slots], 1)
        hg = sum(lax.dot_general(a, b, NT, preferred_element_type=F32) for a, b in zip(lhs, rhs))
        ds = [lax.dot_general(hidden[c], a, TN, preferred_element_type=F32) for a in lhs]
        hgrad[c] += hg
        for k, s in enumerate(slots):
            gsum[s] = ds[k // 2][:, (k % 2) * BLK : (k % 2) * BLK + BLK].astype(BF)

    in_pairs(steps, middle)
    stores = store(grads, gsum, sems, 0)

    def cotangents(c, _):
        g = gu[c, :, :BLK]
        s = jax.nn.sigmoid(g)
        hg = hgrad[c]
        gucot[c, :, :BLK] = (hg * gu[c, :, BLK:] * s * (1.0 + g * (1.0 - s))).astype(BF)
        gucot[c, :, BLK:] = (hg * (g * s)).astype(BF)
        return 0

    lax.fori_loop(0, 7, cotangents, 0)

    def backward(i):
        slots, spots, c = step(table, i, 2)
        d = gucot[c]
        rhs = side([weights[s, :, GU] for s in slots], 0)
        ds = [lax.dot_general(d, b, NT, preferred_element_type=F32) for b in rhs]
        for k, t in enumerate(spots):
            rows[t] += ds[k // 2][:, (k % 2) * BLK : (k % 2) * BLK + BLK]

    in_pairs(steps, backward)
    wait(stores + settle(rows, sums, outs, sems, 5))


def grad_shapes(width):
    return [jax.ShapeDtypeStruct((n, BLK, width), BF) for n in (12, 12, 12, 12, 48)]


def input_work(table, gu, hidden, cot_parts, weights):
    vmem = pltpu.VMEM
    return pl.pallas_call(
        input_body,
        out_shape=part_shapes(256, BLK)
        + grad_shapes(BLK)
        + [jax.ShapeDtypeStruct((7, 256, 2 * BLK), BF)],
        in_specs=[SMEM] + [IN_VMEM] * 2 + [HBM] * 4 + [IN_VMEM],
        out_specs=[HBM] * 9 + [IN_VMEM],
        scratch_shapes=[
            vmem((64, 256, BLK), BF),
            vmem((7, 256, BLK), F32),
            vmem((64, 256, BLK), F32),
            vmem((64, 256, BLK), BF),
            vmem((8 * CAP + 1, BLK, BLK), BF),
            pltpu.SemaphoreType.DMA((14,)),
        ],
        compiler_params=pltpu.CompilerParams(vmem_limit_bytes=24 * MIB),
        cost_estimate=cost(56 * 4 * 4, 22 * MIB),
        name="inputs",
    )(table, gu, hidden, *cot_parts, weights)


def grad_body(table, gucot, *refs):
    token_parts, refs = refs[:4], refs[4:]
    grads, refs = refs[:5], refs[5:]
    acts, gsum, sems = refs
    wait(fetch(token_parts, acts, sems, 0))
    steps = table[4, 0]

    def backward(i):
        slots, spots, c = step(table, i, 1)
        lhs = side([acts[t] for t in spots], 1)
        d = gucot[c]
        res = [lax.dot_general(a, d, TN, preferred_element_type=F32) for a in lhs]
        for k, s in enumerate(slots):
            gsum[s] = res[k // 2][(k % 2) * BLK : (k % 2) * BLK + BLK].astype(BF)

    in_pairs(steps, backward)
    wait(store(grads, gsum, sems, 0))


def grad_work(table, gucot, token_parts):
    vmem = pltpu.VMEM
    return pl.pallas_call(
        grad_body,
        out_shape=grad_shapes(2 * BLK),
        in_specs=[SMEM, IN_VMEM] + [HBM] * 4,
        out_specs=[HBM] * 5,
        scratch_shapes=[
            vmem((64, 256, BLK), BF),
            vmem((8 * CAP + 1, BLK, 2 * BLK), BF),
            pltpu.SemaphoreType.DMA((5,)),
        ],
        compiler_params=pltpu.CompilerParams(vmem_limit_bytes=14 * MIB),
        cost_estimate=cost(56 * 2 * 4, 10 * MIB),
        name="grads",
    )(table, gucot, *token_parts)


def zero_body(*outs):
    for out in outs:
        out[...] = jnp.zeros(out.shape, BF)


def zeros(*shapes):
    return pl.pallas_call(
        zero_body,
        out_shape=[jax.ShapeDtypeStruct(s, BF) for s in shapes],
        name="zeros",
    )()


def unpack_body(mask, where, *refs):
    downs, refs = refs[:4], refs[4:]
    pairs, refs = refs[:4], refs[4:]
    gate, up, down, total, sems = refs[3:]
    row = where[0] * 2 + where[1]
    col = where[2] * 4 + where[3]
    for s in range(CAP):
        for parts, lanes in ((pairs, slice(0, 2 * BLK)), (downs, slice(2 * BLK, 3 * BLK))):
            v = parts[0][s].astype(F32)
            for part in parts[1:]:
                v = v + part[s].astype(F32)
            total[s, :, lanes] = v.astype(BF)

    def copies(slot, i, j):
        r = pl.ds(pl.multiple_of(i * BLK, BLK), BLK)
        c = pl.ds(pl.multiple_of(j * BLK, BLK), BLK)
        return (
            pltpu.make_async_copy(total.at[slot, :, pl.ds(0, BLK)], gate.at[r, c], sems.at[slot, 0]),
            pltpu.make_async_copy(total.at[slot, :, pl.ds(BLK, BLK)], up.at[r, c], sems.at[slot, 1]),
            pltpu.make_async_copy(
                total.at[slot, :, pl.ds(2 * BLK, BLK)], down.at[c, r], sems.at[slot, 2]
            ),
        )

    def tile_col(j, n):
        for i in range(8):
            m = mask[row * 8 + i, col * 7 + j]

            @pl.when((m != 0) & (n < CAP))
            def _(n=n, i=i):
                for copy in copies(n, i, j):
                    copy.start()

            n = n + m
        return n

    n = lax.fori_loop(0, 7, tile_col, jnp.int32(0))

    def finish(s, _):
        for copy in copies(s, 0, 0):
            copy.wait()
        return 0

    lax.fori_loop(0, jnp.minimum(n, CAP), finish, 0)


def unpack(mask, where, downs, pairs, blanks):
    return pl.pallas_call(
        unpack_body,
        out_shape=[jax.ShapeDtypeStruct(v.shape, BF) for v in blanks],
        in_specs=[SMEM, SMEM] + [IN_VMEM] * 8 + [HBM] * 3,
        out_specs=[HBM, HBM, HBM],
        scratch_shapes=[
            pltpu.VMEM((CAP, BLK, 3 * BLK), BF),
            pltpu.SemaphoreType.DMA((CAP, 3)),
        ],
        input_output_aliases={10: 0, 11: 1, 12: 2},
        name="unpack",
    )(mask, where, *downs, *pairs, *blanks)


def on_device(tokens, cotangent, gate_weight, up_weight, down_weight, tile_mask):
    row = lax.axis_index("row")
    col = lax.axis_index("col")
    where = jnp.stack([row // 2, row % 2, col // 4, col % 4]).astype(jnp.int32)

    packed = pack(tile_mask, where, gate_weight, up_weight, down_weight)
    table = plan(tile_mask, where)

    def gather(v, first, second):
        own = jnp.stack([v[:, k * BLK : k * BLK + BLK] for k in range(4)], 0)
        line = jnp.concatenate(gather_four(own, first), 0)
        return gather_four(line, second)

    def finish(got, axis):
        line = [add(*(v[k * 4 : k * 4 + 4] for v in got)) for k in range(4)]
        end = add(*scatter_four(line, axis))
        return jnp.concatenate([end[k] for k in range(4)], 1)

    def row_sums(grads):
        pair = send(grads[4], "core", 1)
        return [add(v, pair[k * CAP : k * CAP + CAP]) for k, v in enumerate(grads[:4])]

    token_parts = gather(tokens, "x", "y")
    a, b, c, d = ring_gather(packed, "z")
    mine = [packed, a, b, c, d]
    weight_parts = mine + [send(v, "core", 1) for v in mine]
    weights = stage(weight_parts)
    cot_parts = gather(cotangent, "y", "x")

    *outs, gu, hidden = forward_work(table, token_parts, weights)
    outs = scatter_four(outs, "y")
    res = input_work(table, gu, hidden, cot_parts, weights)
    ins, downs, gucot = res[:4], res[4:9], res[9]
    ins = scatter_four(ins, "x")
    downs = scatter_four(row_sums(downs), "z")
    pairs = grad_work(table, gucot, token_parts)
    pairs = scatter_four(row_sums(pairs), "z")
    output = finish(outs, "x")
    blanks = zeros(gate_weight.shape, up_weight.shape, down_weight.shape)
    gate_grad, up_grad, down_grad = unpack(tile_mask, where, downs, pairs, blanks)
    input_grad = finish(ins, "y")
    return output, input_grad, gate_grad, up_grad, down_grad


def solution(mesh):
    spec = P("row", "col")
    turned = P("col", "row")

    return jax.shard_map(
        on_device,
        mesh=mesh,
        in_specs=(spec, spec, spec, spec, turned, P()),
        out_specs=(spec, spec, spec, spec, turned),
        check_vma=False,
    )
```

```python
import jax
import jax.numpy as jnp
from jax import lax
from jax.experimental import pallas as pl
from jax.experimental.pallas import tpu as pltpu
from jax.sharding import PartitionSpec as P


BLK = 128
CAP = 12
UNROLL = 4
BF = jnp.bfloat16
F32 = jnp.float32
DIST = (0, 3, 1, 2)
MIB = 1 << 20


def shift(axis, k):
    perm = []
    for r in range(8):
        for c in range(16):
            at = {"z": r // 2, "core": r % 2, "x": c // 4, "y": c % 4}
            at[axis] = (at[axis] + k) % (2 if axis == "core" else 4)
            perm.append((r * 16 + c, (at["z"] * 2 + at["core"]) * 16 + at["x"] * 4 + at["y"]))
    return perm


def send(v, axis, k):
    return lax.ppermute(v, ("row", "col"), shift(axis, k))


def ring_gather(v, axis):
    h = v.shape[0] // 2
    a = send(v, axis, 1)
    b = send(v, axis, -1)
    c, d = a[:h], b[h:]
    return a, b, send(c, axis, 1), send(d, axis, -1)


def gather_four(v, axis):
    return [v, send(v, axis, 1), send(v, axis, -1), send(v, axis, 2)]


def scatter_four(parts, axis):
    own, minus, plus, far = parts
    return [own, send(minus, axis, -1), send(plus, axis, 1), send(far, axis, 2)]


def add(*vs):
    total = vs[0].astype(F32)
    for v in vs[1:]:
        total = total + v.astype(F32)
    return total.astype(BF)


def place(d):
    return jnp.where(d == 0, 0, jnp.where(d == 1, 2, jnp.where(d == 2, 3, 1)))


def place_back(p):
    return jnp.where(p == 0, 0, jnp.where(p == 1, 3, jnp.where(p == 2, 1, 2)))


def pack_body(mask, where, gate, up, down, out, sems):
    row = where[0] * 2 + where[1]
    col = where[2] * 4 + where[3]

    def copies(slot, i, j):
        r = pl.ds(pl.multiple_of(i * BLK, BLK), BLK)
        c = pl.ds(pl.multiple_of(j * BLK, BLK), BLK)
        return (
            pltpu.make_async_copy(gate.at[r, c], out.at[slot, :, pl.ds(0, BLK)], sems.at[slot, 0]),
            pltpu.make_async_copy(up.at[r, c], out.at[slot, :, pl.ds(BLK, BLK)], sems.at[slot, 1]),
            pltpu.make_async_copy(
                down.at[c, r], out.at[slot, :, pl.ds(2 * BLK, BLK)], sems.at[slot, 2]
            ),
        )

    def tile_col(j, n):
        for i in range(8):
            m = mask[row * 8 + i, col * 7 + j]

            @pl.when((m != 0) & (n < CAP))
            def _(n=n, i=i):
                for copy in copies(n, i, j):
                    copy.start()

            n = n + m
        return n

    n = lax.fori_loop(0, 7, tile_col, jnp.int32(0))

    def finish(s, _):
        for copy in copies(s, 0, 0):
            copy.wait()
        return 0

    lax.fori_loop(0, jnp.minimum(n, CAP), finish, 0)


def pack(mask, where, gate, up, down):
    smem = pl.BlockSpec(memory_space=pltpu.SMEM)
    hbm = pl.BlockSpec(memory_space=pltpu.HBM)
    return pl.pallas_call(
        pack_body,
        out_shape=jax.ShapeDtypeStruct((CAP, BLK, 3 * BLK), BF),
        in_specs=[smem, smem, hbm, hbm, hbm],
        out_specs=pl.BlockSpec(memory_space=pltpu.VMEM),
        scratch_shapes=[pltpu.SemaphoreType.DMA((CAP, 3))],
        compiler_params=pltpu.CompilerParams(vmem_limit_bytes=4 * MIB),
        name="pack",
    )(mask, where, gate, up, down)


def plan_body(mask, where, table):
    z, core, x, y = where[0], where[1], where[2], where[3]
    col = x * 4 + y

    def spot(k, _):
        q = k // 8
        d = place_back(q % 4)
        owner = (((z + d) & 3) * 2 + (core ^ (q // 4))) * 2 + (k % 8) // 4
        px = place((owner // 4 - x) & 3)
        py = place((owner % 4 - y) & 3)
        table[5, k] = (py * 4 + px) * 4 + k % 4
        table[6, k] = (px * 4 + py) * 4 + k % 4
        return 0

    lax.fori_loop(0, 64, spot, 0)
    groups = [((z + DIST[q % 4]) & 3) * 2 + (core ^ (q // 4)) for q in range(8)]

    def tile_col(j, carry):
        total, slots = carry[0], list(carry[1:])
        for q in range(8):
            for i in range(8):
                m = mask[groups[q] * 8 + i, col * 7 + j]
                table[0, total] = slots[q]
                table[1, total] = table[5, q * 8 + i]
                table[2, total] = table[6, q * 8 + i]
                table[3, total] = j
                slots[q] = slots[q] + m
                total = total + m
        for k in range(UNROLL):
            table[0, total + k] = 8 * CAP
            table[1, total + k] = 0
            table[2, total + k] = 0
            table[3, total + k] = j
        total = ((total + (UNROLL - 1)) // UNROLL) * UNROLL
        return (total, *slots)

    start = (jnp.int32(0), *(jnp.int32(q * CAP) for q in range(8)))
    total = lax.fori_loop(0, 7, tile_col, start)[0]
    for k in range(UNROLL):
        table[0, total + k] = 8 * CAP
        table[1, total + k] = 0
        table[2, total + k] = 0
        table[3, total + k] = 0
    table[4, 0] = (total // UNROLL + 1) // 2


def plan(mask, where):
    smem = pl.BlockSpec(memory_space=pltpu.SMEM)
    return pl.pallas_call(
        plan_body,
        out_shape=jax.ShapeDtypeStruct((8, 128), jnp.int32),
        in_specs=[smem, smem],
        out_specs=smem,
        compiler_params=pltpu.CompilerParams(vmem_limit_bytes=2 * MIB),
        name="plan",
    )(mask, where)


SMEM = pl.BlockSpec(memory_space=pltpu.SMEM)
HBM = pl.BlockSpec(memory_space=pl.ANY)
IN_VMEM = pl.BlockSpec(memory_space=pltpu.VMEM)
NT = (((1,), (1,)), ((), ()))
TN = (((0,), (0,)), ((), ()))


def fetch(parts, buffer, sems, first):
    copies = []
    at = 0
    for ref in parts:
        n = ref.shape[0]
        copies.append(pltpu.make_async_copy(ref, buffer.at[pl.ds(at, n)], sems.at[first + len(copies)]))
        at += n
    for copy in copies:
        copy.start()
    return copies


def store(parts, buffer, sems, first):
    copies = []
    at = 0
    for ref in parts:
        n = ref.shape[0]
        copies.append(pltpu.make_async_copy(buffer.at[pl.ds(at, n)], ref, sems.at[first + len(copies)]))
        at += n
    for copy in copies:
        copy.start()
    return copies


def wait(copies):
    for copy in copies:
        copy.wait()


def clear(ref):
    def body(p, _):
        ref[p] = jnp.zeros(ref.shape[1:], ref.dtype)
        return 0

    lax.fori_loop(0, ref.shape[0], body, 0)


def settle(rows, sums, parts, sems, first):
    copies = []
    for k, part in enumerate(parts):
        def body(p, _):
            for r in range(4):
                sums[p * 4 + r] = rows[p * 4 + r].astype(BF)
            return 0

        lax.fori_loop(k * 4, k * 4 + 4, body, 0)
        copies.append(pltpu.make_async_copy(sums.at[pl.ds(k * 16, 16)], part, sems.at[first + k]))
        copies[-1].start()
    return copies


def step(table, i, spots):
    at = i * UNROLL
    return (
        [table[0, at + k] for k in range(UNROLL)],
        [table[spots, at + k] for k in range(UNROLL)],
        table[3, at],
    )


def side(values, axis):
    return [jnp.concatenate(values[k : k + 2], axis) for k in range(0, UNROLL, 2)]


GU = slice(0, 2 * BLK)
DOWN = slice(2 * BLK, 3 * BLK)


def stage_body(*refs):
    parts, out, sems = refs[:10], refs[10], refs[11]
    copies = fetch(parts, out, sems, 0)
    out[8 * CAP] = jnp.zeros((BLK, 3 * BLK), BF)
    wait(copies)


def stage(parts):
    return pl.pallas_call(
        stage_body,
        out_shape=jax.ShapeDtypeStruct((8 * CAP + 1, BLK, 3 * BLK), BF),
        in_specs=[HBM] * 10,
        out_specs=IN_VMEM,
        scratch_shapes=[pltpu.SemaphoreType.DMA((10,))],
        compiler_params=pltpu.CompilerParams(vmem_limit_bytes=12 * MIB),
        name="stage",
    )(*parts)


def in_pairs(steps, body):
    def turn(i, _):
        body(i * 2)
        body(i * 2 + 1)
        return 0

    lax.fori_loop(0, steps, turn, 0)


def forward_body(table, *refs):
    token_parts, refs = refs[:4], refs[4:]
    weights, refs = refs[0], refs[1:]
    outs, refs = refs[:4], refs[4:]
    gu, hidden, acts, rows, sums, sems = refs
    loads = fetch(token_parts, acts, sems, 0)
    clear(gu)
    clear(rows)
    wait(loads)
    steps = table[4, 0]

    def forward(i):
        slots, spots, c = step(table, i, 1)
        lhs = side([acts[t] for t in spots], 1)
        rhs = side([weights[s, :, GU] for s in slots], 0)
        gu[c] += sum(jnp.dot(a, b, preferred_element_type=F32) for a, b in zip(lhs, rhs))

    in_pairs(steps, forward)

    def activate(c, _):
        g = gu[c, :, :BLK]
        hidden[c] = (g * jax.nn.sigmoid(g) * gu[c, :, BLK:]).astype(BF)
        return 0

    lax.fori_loop(0, 7, activate, 0)

    def output(i):
        slots, spots, c = step(table, i, 1)
        h = hidden[c]
        rhs = side([weights[s, :, DOWN] for s in slots], 1)
        ds = [jnp.dot(h, b, preferred_element_type=F32) for b in rhs]
        for k, t in enumerate(spots):
            rows[t] += ds[k // 2][:, (k % 2) * BLK : (k % 2) * BLK + BLK]

    in_pairs(steps, output)
    wait(settle(rows, sums, outs, sems, 0))


def cost(tiles, moved):
    return pl.CostEstimate(
        flops=tiles * 8 * 2 * 256 * BLK * BLK, bytes_accessed=moved, transcendentals=0
    )


def part_shapes(*tail):
    return [jax.ShapeDtypeStruct((16, *tail), BF)] * 4


def forward_work(table, token_parts, weights):
    vmem = pltpu.VMEM
    return pl.pallas_call(
        forward_body,
        out_shape=part_shapes(256, BLK)
        + [jax.ShapeDtypeStruct((7, 256, 2 * BLK), F32), jax.ShapeDtypeStruct((7, 256, BLK), BF)],
        in_specs=[SMEM] + [HBM] * 4 + [IN_VMEM],
        out_specs=[HBM] * 4 + [IN_VMEM] * 2,
        scratch_shapes=[
            vmem((64, 256, BLK), BF),
            vmem((64, 256, BLK), F32),
            vmem((64, 256, BLK), BF),
            pltpu.SemaphoreType.DMA((14,)),
        ],
        compiler_params=pltpu.CompilerParams(vmem_limit_bytes=20 * MIB),
        cost_estimate=cost(56 * 3 * 4, 20 * MIB),
        name="forward",
    )(table, *token_parts, weights)


def input_body(table, gu, hidden, *refs):
    cot_parts, refs = refs[:4], refs[4:]
    weights, refs = refs[0], refs[1:]
    outs, refs = refs[:4], refs[4:]
    grads, refs = refs[:5], refs[5:]
    gucot, cots, hgrad, rows, sums, gsum, sems = refs
    loads = fetch(cot_parts, cots, sems, 0)
    clear(hgrad)
    clear(rows)
    wait(loads)
    steps = table[4, 0]

    def middle(i):
        slots, spots, c = step(table, i, 2)
        gs = [cots[t] for t in spots]
        lhs = side(gs, 1)
        rhs = side([weights[s, :, DOWN] for s in slots], 1)
        hg = sum(lax.dot_general(a, b, NT, preferred_element_type=F32) for a, b in zip(lhs, rhs))
        ds = [lax.dot_general(hidden[c], a, TN, preferred_element_type=F32) for a in lhs]
        hgrad[c] += hg
        for k, s in enumerate(slots):
            gsum[s] = ds[k // 2][:, (k % 2) * BLK : (k % 2) * BLK + BLK].astype(BF)

    in_pairs(steps, middle)
    stores = store(grads, gsum, sems, 0)

    def cotangents(c, _):
        g = gu[c, :, :BLK]
        s = jax.nn.sigmoid(g)
        hg = hgrad[c]
        gucot[c, :, :BLK] = (hg * gu[c, :, BLK:] * s * (1.0 + g * (1.0 - s))).astype(BF)
        gucot[c, :, BLK:] = (hg * (g * s)).astype(BF)
        return 0

    lax.fori_loop(0, 7, cotangents, 0)

    def backward(i):
        slots, spots, c = step(table, i, 2)
        d = gucot[c]
        rhs = side([weights[s, :, GU] for s in slots], 0)
        ds = [lax.dot_general(d, b, NT, preferred_element_type=F32) for b in rhs]
        for k, t in enumerate(spots):
            rows[t] += ds[k // 2][:, (k % 2) * BLK : (k % 2) * BLK + BLK]

    in_pairs(steps, backward)
    wait(stores + settle(rows, sums, outs, sems, 5))


def grad_shapes(width):
    return [jax.ShapeDtypeStruct((n, BLK, width), BF) for n in (12, 12, 12, 12, 48)]


def input_work(table, gu, hidden, cot_parts, weights):
    vmem = pltpu.VMEM
    return pl.pallas_call(
        input_body,
        out_shape=part_shapes(256, BLK)
        + grad_shapes(BLK)
        + [jax.ShapeDtypeStruct((7, 256, 2 * BLK), BF)],
        in_specs=[SMEM] + [IN_VMEM] * 2 + [HBM] * 4 + [IN_VMEM],
        out_specs=[HBM] * 9 + [IN_VMEM],
        scratch_shapes=[
            vmem((64, 256, BLK), BF),
            vmem((7, 256, BLK), F32),
            vmem((64, 256, BLK), F32),
            vmem((64, 256, BLK), BF),
            vmem((8 * CAP + 1, BLK, BLK), BF),
            pltpu.SemaphoreType.DMA((14,)),
        ],
        compiler_params=pltpu.CompilerParams(vmem_limit_bytes=24 * MIB),
        cost_estimate=cost(56 * 4 * 4, 22 * MIB),
        name="inputs",
    )(table, gu, hidden, *cot_parts, weights)


def grad_body(table, gucot, *refs):
    token_parts, refs = refs[:4], refs[4:]
    grads, refs = refs[:5], refs[5:]
    acts, gsum, sems = refs
    wait(fetch(token_parts, acts, sems, 0))
    steps = table[4, 0]

    def backward(i):
        slots, spots, c = step(table, i, 1)
        lhs = side([acts[t] for t in spots], 1)
        d = gucot[c]
        res = [lax.dot_general(a, d, TN, preferred_element_type=F32) for a in lhs]
        for k, s in enumerate(slots):
            gsum[s] = res[k // 2][(k % 2) * BLK : (k % 2) * BLK + BLK].astype(BF)

    in_pairs(steps, backward)
    wait(store(grads, gsum, sems, 0))


def grad_work(table, gucot, token_parts):
    vmem = pltpu.VMEM
    return pl.pallas_call(
        grad_body,
        out_shape=grad_shapes(2 * BLK),
        in_specs=[SMEM, IN_VMEM] + [HBM] * 4,
        out_specs=[HBM] * 5,
        scratch_shapes=[
            vmem((64, 256, BLK), BF),
            vmem((8 * CAP + 1, BLK, 2 * BLK), BF),
            pltpu.SemaphoreType.DMA((5,)),
        ],
        compiler_params=pltpu.CompilerParams(vmem_limit_bytes=14 * MIB),
        cost_estimate=cost(56 * 2 * 4, 10 * MIB),
        name="grads",
    )(table, gucot, *token_parts)


def zero_body(*outs):
    for out in outs:
        out[...] = jnp.zeros(out.shape, BF)


def zeros(*shapes):
    return pl.pallas_call(
        zero_body,
        out_shape=[jax.ShapeDtypeStruct(s, BF) for s in shapes],
        compiler_params=pltpu.CompilerParams(vmem_limit_bytes=8 * MIB),
        name="zeros",
    )()


def unpack_body(mask, where, *refs):
    downs, refs = refs[:4], refs[4:]
    pairs, refs = refs[:4], refs[4:]
    gate, up, down, total, sems = refs[3:]
    row = where[0] * 2 + where[1]
    col = where[2] * 4 + where[3]
    for s in range(CAP):
        for parts, lanes in ((pairs, slice(0, 2 * BLK)), (downs, slice(2 * BLK, 3 * BLK))):
            v = parts[0][s].astype(F32)
            for part in parts[1:]:
                v = v + part[s].astype(F32)
            total[s, :, lanes] = v.astype(BF)

    def copies(slot, i, j):
        r = pl.ds(pl.multiple_of(i * BLK, BLK), BLK)
        c = pl.ds(pl.multiple_of(j * BLK, BLK), BLK)
        return (
            pltpu.make_async_copy(total.at[slot, :, pl.ds(0, BLK)], gate.at[r, c], sems.at[slot, 0]),
            pltpu.make_async_copy(total.at[slot, :, pl.ds(BLK, BLK)], up.at[r, c], sems.at[slot, 1]),
            pltpu.make_async_copy(
                total.at[slot, :, pl.ds(2 * BLK, BLK)], down.at[c, r], sems.at[slot, 2]
            ),
        )

    def tile_col(j, n):
        for i in range(8):
            m = mask[row * 8 + i, col * 7 + j]

            @pl.when((m != 0) & (n < CAP))
            def _(n=n, i=i):
                for copy in copies(n, i, j):
                    copy.start()

            n = n + m
        return n

    n = lax.fori_loop(0, 7, tile_col, jnp.int32(0))

    def finish(s, _):
        for copy in copies(s, 0, 0):
            copy.wait()
        return 0

    lax.fori_loop(0, jnp.minimum(n, CAP), finish, 0)


def unpack(mask, where, downs, pairs, blanks):
    return pl.pallas_call(
        unpack_body,
        out_shape=[jax.ShapeDtypeStruct(v.shape, BF) for v in blanks],
        in_specs=[SMEM, SMEM] + [IN_VMEM] * 8 + [HBM] * 3,
        out_specs=[HBM, HBM, HBM],
        scratch_shapes=[
            pltpu.VMEM((CAP, BLK, 3 * BLK), BF),
            pltpu.SemaphoreType.DMA((CAP, 3)),
        ],
        input_output_aliases={10: 0, 11: 1, 12: 2},
        compiler_params=pltpu.CompilerParams(vmem_limit_bytes=10 * MIB),
        name="unpack",
    )(mask, where, *downs, *pairs, *blanks)


def on_device(tokens, cotangent, gate_weight, up_weight, down_weight, tile_mask):
    row = lax.axis_index("row")
    col = lax.axis_index("col")
    where = jnp.stack([row // 2, row % 2, col // 4, col % 4]).astype(jnp.int32)

    packed = pack(tile_mask, where, gate_weight, up_weight, down_weight)
    table = plan(tile_mask, where)

    def gather(v, first, second):
        own = jnp.stack([v[:, k * BLK : k * BLK + BLK] for k in range(4)], 0)
        line = jnp.concatenate(gather_four(own, first), 0)
        return gather_four(line, second)

    def finish(got, axis):
        line = [add(*(v[k * 4 : k * 4 + 4] for v in got)) for k in range(4)]
        end = add(*scatter_four(line, axis))
        return jnp.concatenate([end[k] for k in range(4)], 1)

    def row_sums(grads):
        pair = send(grads[4], "core", 1)
        return [add(v, pair[k * CAP : k * CAP + CAP]) for k, v in enumerate(grads[:4])]

    token_parts = gather(tokens, "x", "y")
    a, b, c, d = ring_gather(packed, "z")
    mine = [packed, a, b, c, d]
    weight_parts = mine + [send(v, "core", 1) for v in mine]
    weights = stage(weight_parts)
    cot_parts = gather(cotangent, "y", "x")

    *outs, gu, hidden = forward_work(table, token_parts, weights)
    outs = scatter_four(outs, "y")
    res = input_work(table, gu, hidden, cot_parts, weights)
    ins, downs, gucot = res[:4], res[4:9], res[9]
    ins = scatter_four(ins, "x")
    downs = scatter_four(row_sums(downs), "z")
    pairs = grad_work(table, gucot, token_parts)
    pairs = scatter_four(row_sums(pairs), "z")
    output = finish(outs, "x")
    blanks = zeros(gate_weight.shape, up_weight.shape, down_weight.shape)
    gate_grad, up_grad, down_grad = unpack(tile_mask, where, downs, pairs, blanks)
    input_grad = finish(ins, "y")
    return output, input_grad, gate_grad, up_grad, down_grad


def solution(mesh):
    spec = P("row", "col")
    turned = P("col", "row")

    return jax.shard_map(
        on_device,
        mesh=mesh,
        in_specs=(spec, spec, spec, spec, turned, P()),
        out_specs=(spec, spec, spec, spec, turned),
        check_vma=False,
    )
```
